256 devices in a mesh: samp: 8 (over x, core), pos: 32 (over z, y).
Axes of the slice: x: 4, y: 4, z: 8, core: 2. Of those that a mesh axis runs over, the one named last changes fastest.
Arguments:
- dosages: bfloat16 [32768, 32768], P('samp', 'pos'), may hold values from -64 to 64
- phenotypes: bfloat16 [32768, 12288], P('samp', 'pos'), may hold values from -64 to 64
- window_low: int32 [12288], P('pos'), may hold values from 0 to 32767, as said below
- window_high: int32 [12288], P('pos'), may hold values from 0 to 32767, as said below
Outputs:
- statistics: float32 [32, 2048, 384], P('pos', 'samp')
The draws below stay inside these ranges and needn't reach their ends.
Inputs may be any that keep to these rules, and one draw needn't show every extreme that they name: For peak p in block b = p // 384: b * 1024 - 512 <= window_low[p] <= window_high[p] <= b * 1024 + 1535. In every block but the first, one window starts exactly 512 variants before the block; in every block but the last, one ends exactly 512 variants after it. Same bounds as window_low; window_high[p] >= window_low[p].
All inputs are finite; a program needn't handle non-finite values.
Results may differ from the reference program's by a relative error of at most 0.0003.
Values may be sent and summed in bfloat16 or wider, within the bound.
A program may use at most 64 MiB of HBM per device.

```python
import math
import jax
import jax.numpy as jnp
from jax import lax

V_DEV = 1024
P_DEV = 384
HALO = 512
SPAN = 2048
BLOCKS = 32
SAMPLES = 32768
VARIANTS = 32768
PEAKS = 12288


def draw_field(key, row_count, col_count):
    key_base, key_cols, key_rows = jax.random.split(key, 3)
    base = jax.random.truncated_normal(key_base, -4.0, 4.0, (row_count, col_count), jnp.float32)
    col_scale = jnp.exp(jax.random.uniform(key_cols, (1, col_count), jnp.float32, jnp.log(0.3), jnp.log(3.0)))
    position = jnp.arange(row_count, dtype=jnp.float32)[:, None] / row_count
    row_mix = 0.5 * position + 0.5 * jax.random.uniform(key_rows, (row_count, 1), jnp.float32)
    row_scale = jnp.exp(jnp.log(0.4) + jnp.log(10.0) * row_mix)
    field = base * row_scale * col_scale
    return field


def draw_dosages(key, part):
    return draw_field(jax.random.fold_in(key, 11), SAMPLES, VARIANTS).astype(jnp.bfloat16)


def draw_phenotypes(key, part):
    return draw_field(jax.random.fold_in(key, 13), SAMPLES, PEAKS).astype(jnp.bfloat16)


def draw_windows(key):
    key_centre, key_left, key_right = jax.random.split(jax.random.fold_in(key, 7), 3)
    peak_index = jnp.arange(PEAKS, dtype=jnp.int32)
    block_index = peak_index // P_DEV
    local_index = peak_index % P_DEV
    block_first = block_index * V_DEV
    centre = block_first + jax.random.randint(key_centre, (PEAKS,), 0, V_DEV, dtype=jnp.int32)
    left_reach = jax.random.randint(key_left, (PEAKS,), HALO // 8, HALO + 1, dtype=jnp.int32)
    right_reach = jax.random.randint(key_right, (PEAKS,), HALO // 8, HALO + 1, dtype=jnp.int32)
    is_first = local_index == 0
    is_last = local_index == P_DEV - 1
    centre = jnp.where(is_first, block_first, jnp.where(is_last, block_first + V_DEV - 1, centre))
    left_reach = jnp.where(is_first, HALO, left_reach)
    right_reach = jnp.where(is_last, HALO, right_reach)
    lows = jnp.maximum(centre - left_reach, 0)
    highs = jnp.minimum(centre + right_reach, VARIANTS - 1)
    return (lows.astype(jnp.int32), highs.astype(jnp.int32))


def draw_window_low(key, part):
    return draw_windows(key)[0]


def draw_window_high(key, part):
    return draw_windows(key)[1]


def setup_inputs(seed: int = 0) -> dict:
    key_of = jax.random.split(jax.random.key(seed), 5)
    dosages = draw_dosages(jax.random.fold_in(key_of[4], 71), 0)
    phenotypes = draw_phenotypes(jax.random.fold_in(key_of[4], 71), 0)
    window_low = draw_window_low(jax.random.fold_in(key_of[4], 71), 0)
    window_high = draw_window_high(jax.random.fold_in(key_of[4], 71), 0)
    return {"dosages": dosages, "phenotypes": phenotypes, "window_low": window_low, "window_high": window_high}


EPS = 1e-06

def sum_squares(values):
    return lax.optimization_barrier(jnp.sum(jnp.square(values.astype(jnp.float32)), axis=0))

def reference(dosages, phenotypes, window_low, window_high):
    padded = jnp.pad(dosages, ((0, 0), (HALO, HALO)))
    factor = math.sqrt(float(SAMPLES - 2))

    def one_block(block_index):
        variant_panel = lax.dynamic_slice_in_dim(padded, (block_index * V_DEV).astype(jnp.int32), SPAN, 1)
        peak_panel = lax.dynamic_slice_in_dim(phenotypes, (block_index * P_DEV).astype(jnp.int32), P_DEV, 1)
        lows = lax.dynamic_slice_in_dim(window_low, (block_index * P_DEV).astype(jnp.int32), P_DEV, 0)
        highs = lax.dynamic_slice_in_dim(window_high, (block_index * P_DEV).astype(jnp.int32), P_DEV, 0)
        cross = lax.dot_general(variant_panel, peak_panel, (((0,), (0,)), ((), ())), preferred_element_type=jnp.float32)
        variant_squares = sum_squares(variant_panel)
        peak_squares = sum_squares(peak_panel)
        variant_index = block_index * V_DEV - HALO + jnp.arange(SPAN, dtype=jnp.int32)[:, None]
        inside = (variant_index >= lows[None, :]) & (variant_index <= highs[None, :])
        scale_terms = (variant_squares[:, None] + EPS) * (peak_squares[None, :] + EPS)
        statistic = factor * cross / jnp.sqrt(scale_terms)
        return jnp.where(inside, statistic, jnp.zeros_like(statistic))
    return lax.map(one_block, jnp.arange(BLOCKS, dtype=jnp.int32))
```

```python
import functools
import math

import jax
import jax.numpy as jnp
from jax import lax
from jax.experimental import pallas as pl
from jax.experimental.pallas import tpu as pltpu
from jax.sharding import PartitionSpec as P

HALO = 512
EPS = 1e-06
MESH = pl.DeviceIdType.MESH

PIECE = 48
PIECES = 3
CAP = PIECE * PIECES
QUARTER = 256
EXTRA = 8


def padded(cells, sides, width):
    for axis, dim in sides:
        count = lax.axis_size(axis)
        ends = count - 1
        head = lax.slice_in_dim(cells, 0, width, axis=dim)
        tail = lax.slice_in_dim(cells, cells.shape[dim] - width, cells.shape[dim], axis=dim)
        cells = jnp.concatenate(
            [
                lax.ppermute(tail, axis, [(i, (i + 1) % count) for i in range(ends)]),
                cells,
                lax.ppermute(head, axis, [((i + 1) % count, i) for i in range(ends)]),
            ],
            axis=dim,
        )
    return cells


def from_behind(array, axis, by):
    devices = lax.axis_size(axis)
    pairs = [(i, i + by) for i in range(devices) if 0 <= i + by < devices]
    return lax.ppermute(array, axis, pairs)


def sum_squares(values):
    return jnp.sum(jnp.square(values.astype(jnp.float32)), axis=0)


def cross_rows(variant_panel, phenotypes):
    return lax.dot_general(
        variant_panel, phenotypes, (((0,), (0,)), ((), ())), preferred_element_type=jnp.float32
    )


def dense(dosages, phenotypes, window_low, window_high):
    sample_rows, block_width = dosages.shape
    peak_width = phenotypes.shape[1]
    span_width = block_width + 2 * HALO
    samp_count = lax.axis_size("samp")
    samp_index = lax.axis_index("samp")
    pos_index = lax.axis_index("pos")
    share_rows = span_width // samp_count
    own_first = samp_index * share_rows
    near_peaks = padded(phenotypes, (("pos", 1),), peak_width)
    own_tile = cross_rows(dosages, phenotypes)
    lower_edge = cross_rows(dosages[:, :HALO], near_peaks[:, :peak_width])
    upper_edge = cross_rows(dosages[:, block_width - HALO :], near_peaks[:, 2 * peak_width :])
    from_below = from_behind(upper_edge, "pos", 1)
    from_above = from_behind(lower_edge, "pos", -1)
    assembled = jnp.concatenate([from_below, own_tile, from_above], axis=0)
    owned_squares = lax.psum(sum_squares(dosages), "samp")
    peak_total = lax.psum(sum_squares(phenotypes), "samp")
    variant_total = padded(owned_squares, (("pos", 0),), HALO)
    pieces = assembled.reshape(samp_count, share_rows, peak_width)
    cross_share = jnp.sum(lax.all_to_all(pieces, "samp", 0, 0, tiled=True), axis=0)
    variant_share = lax.dynamic_slice_in_dim(variant_total, own_first, share_rows, 0)
    variant_index = (
        pos_index * block_width
        - HALO
        + own_first
        + jnp.arange(share_rows, dtype=jnp.int32)[:, None]
    )
    inside = (variant_index >= window_low[None, :]) & (variant_index <= window_high[None, :])
    factor = math.sqrt(float(sample_rows * samp_count - 2))
    scale_terms = (variant_share[:, None] + EPS) * (peak_total[None, :] + EPS)
    statistic = factor * cross_share / jnp.sqrt(scale_terms)
    return jnp.where(inside, statistic, jnp.zeros_like(statistic))


def squares_by_eight(values):
    wide = jnp.square(values.astype(jnp.float32))
    rows, columns = wide.shape
    return jnp.sum(wide.reshape(rows // EXTRA, EXTRA, columns), axis=0)


def nt(a, b):
    return lax.dot_general(a, b, (((1,), (1,)), ((), ())), preferred_element_type=jnp.float32)


def tn(a, b):
    return lax.dot_general(a, b, (((0,), (0,)), ((), ())), preferred_element_type=jnp.float32)


def nn(a, b):
    return lax.dot_general(a, b, (((1,), (0,)), ((), ())), preferred_element_type=jnp.float32)


def packed_kernel(
    blocks,
    factor,
    d_hbm,
    p_hbm,
    low_ref,
    high_ref,
    out_ref,
    d,
    p,
    pt,
    pick,
    out_sel,
    in_sel,
    own,
    own0,
    own1,
    own2,
    vs8,
    ps_slots,
    edge,
    edge0,
    edge1,
    edge2,
    packed,
    d_sem,
    p_sem,
    sel_send,
    sel_recv,
    ps_send,
    ps_recv,
    own_send,
    own_recv,
    e0_send,
    e0_recv,
    e1_send,
    e1_recv,
    e2_send,
    e2_recv,
):
    samples, variants = d.shape
    peaks = p.shape[1]
    step = samples // d_sem.shape[0]
    steps = d_sem.shape[0]
    half = variants // 2
    s = lax.axis_index("samp")
    b = lax.axis_index("pos")
    x = s // 2
    c = s % 2
    k = x // 2
    odd = x % 2
    above = (b + 1) % blocks
    below = (b + blocks - 1) % blocks
    sibling = {"samp": x * 2 + 1 - c, "pos": b}
    across = {"samp": (3 - x) * 2 + c, "pos": b}
    beside = {"samp": (x + 1 - 2 * odd) * 2 + c, "pos": b}

    def p_copy(i):
        rows = pl.ds(pl.multiple_of(i * step, step), step)
        return pltpu.make_async_copy(p_hbm.at[rows], p.at[rows], p_sem.at[i])

    def d_copy(i):
        rows = pl.ds(pl.multiple_of(i * step, step), step)
        return pltpu.make_async_copy(d_hbm.at[rows], d.at[rows], d_sem.at[i])

    barrier = pltpu.get_barrier_semaphore()

    def greet(samp, pos):
        pl.semaphore_signal(
            barrier, inc=1, device_id={"samp": samp, "pos": pos}, device_id_type=MESH
        )

    for i in range(steps):
        p_copy(i).start()
    for i in range(steps):
        d_copy(i).start()
    for i in range(1, 8):
        greet((s + i) % 8, b)
    greet(s, above)
    greet(s, below)
    greet((x + 1 - 2 * odd) * 2 + c, (b + blocks + 2 * odd - 1) % blocks)

    first = b * variants
    low = low_ref[...]
    high = high_ref[...]
    before = lax.broadcasted_iota(jnp.int32, (peaks, peaks), 0) < lax.broadcasted_iota(
        jnp.int32, (peaks, peaks), 1
    )
    before = jnp.where(before, 1.0, 0.0).astype(jnp.bfloat16)
    slot = lax.broadcasted_iota(jnp.int32, (CAP, peaks), 0).astype(jnp.float32)
    for side, reach in enumerate((low < first, high >= first + variants)):
        flag = jnp.where(reach, 1.0, 0.0)
        rank = nn(jnp.broadcast_to(flag, (16, peaks)).astype(jnp.bfloat16), before)[0:1]
        rank = jnp.where(reach, rank, -1.0)
        pick[side] = jnp.where(slot == rank, 1.0, 0.0).astype(jnp.bfloat16)

    def select(i, carry):
        p_copy(i).wait()
        rows = pl.ds(pl.multiple_of(i * step, step), step)
        part = p[rows, :]
        for side in range(2):
            got = nt(pick[side], part).astype(jnp.bfloat16)
            for piece in range(PIECES):
                out_sel[side, piece, :, rows] = got[piece * PIECE : (piece + 1) * PIECE]
        return carry

    lax.fori_loop(0, steps, select, 0)
    pl.semaphore_wait(barrier, 10)

    def sel_copy(side, piece):
        return pltpu.make_async_remote_copy(
            src_ref=out_sel.at[side, piece],
            dst_ref=in_sel.at[side, piece],
            send_sem=sel_send.at[side, piece],
            recv_sem=sel_recv.at[side, piece],
            device_id={"samp": s, "pos": (below, above)[side]},
            device_id_type=MESH,
        )

    for piece in range(PIECES):
        for side in range(2):
            sel_copy(side, piece).start()

    same = lax.broadcasted_iota(jnp.int32, (peaks, peaks), 0) == lax.broadcasted_iota(
        jnp.int32, (peaks, peaks), 1
    )
    same = jnp.where(same, 1.0, 0.0).astype(jnp.bfloat16)

    def turn(i, total):
        rows = pl.ds(pl.multiple_of(i * step, step), step)
        part = p[rows, :]
        pt[:, rows] = nt(same, part).astype(jnp.bfloat16)
        return total + squares_by_eight(part)

    ps_slots[s] = lax.fori_loop(0, steps, turn, jnp.zeros((EXTRA, peaks), jnp.float32))

    def ps_copy(i):
        return pltpu.make_async_remote_copy(
            src_ref=ps_slots.at[s],
            dst_ref=ps_slots.at[s],
            send_sem=ps_send.at[i],
            recv_sem=ps_recv.at[s],
            device_id={"samp": (s + i) % 8, "pos": b},
            device_id_type=MESH,
        )

    for i in range(1, 8):
        ps_copy(i).start()

    own[...] = jnp.zeros_like(own)
    vs8[...] = jnp.zeros_like(vs8)

    def multiply(i, carry):
        d_copy(i).wait()
        rows = pl.ds(pl.multiple_of(i * step, step), step)
        part = pt[:, rows]
        for q in range(4):
            columns = slice(q * QUARTER, (q + 1) * QUARTER)
            own[q % 2, q // 2, 0:peaks, :] += nn(part, d[rows, columns])
        vs8[...] += squares_by_eight(d[rows, :])
        return carry

    lax.fori_loop(0, steps, multiply, 0)
    for q in range(4):
        own[q % 2, q // 2, peaks : peaks + EXTRA, :] = vs8[:, q * QUARTER : (q + 1) * QUARTER]

    def own_copy(stage, src, dst, device):
        return pltpu.make_async_remote_copy(
            src_ref=src,
            dst_ref=dst,
            send_sem=own_send.at[stage],
            recv_sem=own_recv.at[stage],
            device_id=device,
            device_id_type=MESH,
        )

    own_a = own_copy(0, own.at[1 - c], own0, sibling)
    own_b = own_copy(1, own0.at[1 - k], own1, across)
    own_c = own_copy(2, own1, own2, beside)

    def e0_copy(piece):
        return pltpu.make_async_remote_copy(
            src_ref=edge.at[piece, 1 - c],
            dst_ref=edge0.at[piece],
            send_sem=e0_send.at[piece],
            recv_sem=e0_recv.at[piece],
            device_id=sibling,
            device_id_type=MESH,
        )

    def e1_copy(piece):
        return pltpu.make_async_remote_copy(
            src_ref=edge0.at[piece, 1 - k],
            dst_ref=edge1.at[piece],
            send_sem=e1_send.at[piece],
            recv_sem=e1_recv.at[piece],
            device_id=across,
            device_id_type=MESH,
        )

    def e2_copy(piece):
        line = (x + k) % 2
        return pltpu.make_async_remote_copy(
            src_ref=edge1.at[piece],
            dst_ref=edge2.at[piece, line],
            send_sem=e2_send.at[piece],
            recv_sem=e2_recv.at[piece, line],
            device_id={"samp": 6 * k + c, "pos": (b + blocks + 1 - 2 * k) % blocks},
            device_id_type=MESH,
        )

    def e2_arrival(piece, line):
        return pltpu.make_async_remote_copy(
            src_ref=edge1.at[piece],
            dst_ref=edge2.at[piece, line],
            send_sem=e2_send.at[piece],
            recv_sem=e2_recv.at[piece, line],
            device_id=sibling,
            device_id_type=MESH,
        )

    def edges(piece):
        for side in range(2):
            sel_copy(side, piece).wait_recv()
        for side in range(2):
            base = half * (1 - side)

            def part(i, total):
                rows = pl.ds(pl.multiple_of(i * step, step), step)
                return total + nn(in_sel[side, piece, :, rows], d[rows, base : base + half])

            got = lax.fori_loop(0, steps, part, jnp.zeros((PIECE, half), jnp.float32))
            for core in range(2):
                columns = slice(core * QUARTER, (core + 1) * QUARTER)
                edge[piece, core, side, 0:PIECE, :] = got[:, columns]
                edge[piece, core, side, PIECE : PIECE + EXTRA, :] = vs8[
                    :, base + core * QUARTER : base + (core + 1) * QUARTER
                ]
        e0_copy(piece).start()

    def edges_by_core(piece):
        e0_copy(piece).wait_recv()
        edge0[piece] = edge0[piece] + edge[piece, c]
        e1_copy(piece).start()

    def edges_by_chip(piece):
        e1_copy(piece).wait_recv()
        edge1[piece] = edge1[piece] + edge0[piece, k]
        e2_copy(piece).start()

    own_a.start()
    edges(0)
    own_a.wait_recv()
    own0[...] = own0[...] + own[c]
    own_b.start()
    edges_by_core(0)
    edges(1)
    edges_by_chip(0)
    edges_by_core(1)
    own_b.wait_recv()
    own1[...] = own1[...] + own0[k]

    @pl.when((x == 0) | (x == 3))
    def _():
        own_c.start()

    edges_by_chip(1)
    edges(2)
    edges_by_core(2)
    edges_by_chip(2)

    for i in range(1, 8):
        sender = (s + i) % 8
        pltpu.make_async_remote_copy(
            src_ref=ps_slots.at[sender],
            dst_ref=ps_slots.at[sender],
            send_sem=ps_send.at[i],
            recv_sem=ps_recv.at[sender],
            device_id=sibling,
            device_id_type=MESH,
        ).wait_recv()
    ps = ps_slots[0]
    for i in range(1, 8):
        ps = ps + ps_slots[i]
    peak_scale = factor / jnp.sqrt(jnp.sum(ps, axis=0, keepdims=True) + EPS)

    def finish(cross):
        index = (
            first
            - HALO
            + s * QUARTER
            + lax.broadcasted_iota(jnp.int32, (QUARTER, peaks), 0)
        )
        inside = (index >= low) & (index <= high)
        out_ref[...] = jnp.where(inside, cross * peak_scale, 0.0)

    def variant_scale(eight):
        return 1.0 / jnp.sqrt(jnp.sum(eight, axis=0, keepdims=True) + EPS)

    @pl.when((x == 1) | (x == 2))
    def _():
        own_c.wait_recv()
        scale = variant_scale(own1[peaks : peaks + EXTRA] + own2[peaks : peaks + EXTRA])
        finish(((own1[0:peaks] + own2[0:peaks]) * scale).T)

    for side in range(2):

        @pl.when(x == 3 * side)
        def _(side=side):
            own_c.wait_send()
            for piece in range(PIECES):
                for line in range(2):
                    e2_arrival(piece, line).wait_recv()
            scale = variant_scale(
                edge2[0, 0, PIECE : PIECE + EXTRA] + edge2[0, 1, PIECE : PIECE + EXTRA]
            )
            for piece in range(PIECES):
                packed[piece * PIECE : (piece + 1) * PIECE, :] = (
                    edge2[piece, 0, 0:PIECE] + edge2[piece, 1, 0:PIECE]
                ) * scale
            rest = packed[...]
            cross = jnp.zeros((QUARTER, peaks), jnp.float32)
            for _ in range(3):
                top = rest.astype(jnp.bfloat16)
                cross = cross + tn(top, pick[side])
                rest = rest - top.astype(jnp.float32)
            finish(cross)

    for piece in range(PIECES):
        for side in range(2):
            sel_copy(side, piece).wait_send()
        e0_copy(piece).wait_send()
        e1_copy(piece).wait_send()
        e2_copy(piece).wait_send()
    for i in range(1, 8):
        ps_copy(i).wait_send()
    own_a.wait_send()
    own_b.wait_send()


def packed_form(dosages, phenotypes, window_low, window_high):
    samples, variants = dosages.shape
    peaks = phenotypes.shape[1]
    steps = 8
    samp_count = lax.axis_size("samp")
    factor = math.sqrt(float(samples * samp_count - 2))
    tall = peaks + EXTRA
    short = PIECE + EXTRA
    f32, bf16 = jnp.float32, jnp.bfloat16
    dma = pltpu.SemaphoreType.DMA
    return pl.pallas_call(
        functools.partial(packed_kernel, lax.axis_size("pos"), factor),
        out_shape=jax.ShapeDtypeStruct((QUARTER, peaks), f32),
        in_specs=[pl.BlockSpec(memory_space=pl.ANY)] * 2
        + [pl.BlockSpec(memory_space=pltpu.VMEM)] * 2,
        out_specs=pl.BlockSpec(memory_space=pltpu.VMEM),
        scratch_shapes=[
            pltpu.VMEM((samples, variants), bf16),
            pltpu.VMEM((samples, peaks), bf16),
            pltpu.VMEM((peaks, samples), bf16),
            pltpu.VMEM((2, CAP, peaks), bf16),
            pltpu.VMEM((2, PIECES, PIECE, samples), bf16),
            pltpu.VMEM((2, PIECES, PIECE, samples), bf16),
            pltpu.VMEM((2, 2, tall, QUARTER), f32),
            pltpu.VMEM((2, tall, QUARTER), f32),
            pltpu.VMEM((tall, QUARTER), f32),
            pltpu.VMEM((tall, QUARTER), f32),
            pltpu.VMEM((EXTRA, variants), f32),
            pltpu.VMEM((8, EXTRA, peaks), f32),
            pltpu.VMEM((PIECES, 2, 2, short, QUARTER), f32),
            pltpu.VMEM((PIECES, 2, short, QUARTER), f32),
            pltpu.VMEM((PIECES, short, QUARTER), f32),
            pltpu.VMEM((PIECES, 2, short, QUARTER), f32),
            pltpu.VMEM((CAP, QUARTER), f32),
            dma((steps,)),
            dma((steps,)),
            dma((2, PIECES)),
            dma((2, PIECES)),
            dma((8,)),
            dma((8,)),
            dma((3,)),
            dma((3,)),
            dma((PIECES,)),
            dma((PIECES,)),
            dma((PIECES,)),
            dma((PIECES,)),
            dma((PIECES,)),
            dma((PIECES, 2)),
        ],
        compiler_params=pltpu.CompilerParams(
            collective_id=0, has_side_effects=True, vmem_limit_bytes=40 << 20
        ),
    )(dosages, phenotypes, window_low[None, :], window_high[None, :])


def shards(dosages, phenotypes, window_low, window_high):
    first = lax.axis_index("pos") * dosages.shape[1]
    count_low = jnp.sum((window_low < first).astype(jnp.int32))
    count_high = jnp.sum((window_high >= first + dosages.shape[1]).astype(jnp.int32))
    most = lax.pmax(jnp.maximum(count_low, count_high), "pos")
    found = packed_form(dosages, phenotypes, window_low, window_high)
    found = lax.cond(
        most > CAP,
        lambda: dense(dosages, phenotypes, window_low, window_high),
        lambda: found,
    )
    return found[None]


def solution(mesh):
    placed = (P("samp", "pos"), P("samp", "pos"), P("pos"), P("pos"))
    return jax.shard_map(
        shards, mesh=mesh, in_specs=placed, out_specs=P("pos", "samp", None), check_vma=False
    )
```

```python
import functools
import math

import jax
import jax.numpy as jnp
from jax import lax
from jax.experimental import pallas as pl
from jax.experimental.pallas import tpu as pltpu
from jax.sharding import PartitionSpec as P

HALO = 512
EPS = 1e-06
MESH = pl.DeviceIdType.MESH

PIECES = (112, 32)
CAP = sum(PIECES)
QUARTER = 256
EXTRA = 8
LANES = 128
STEPS = 8
PARTS = 4


def padded(cells, sides, width):
    for axis, dim in sides:
        count = lax.axis_size(axis)
        ends = count - 1
        head = lax.slice_in_dim(cells, 0, width, axis=dim)
        tail = lax.slice_in_dim(cells, cells.shape[dim] - width, cells.shape[dim], axis=dim)
        cells = jnp.concatenate(
            [
                lax.ppermute(tail, axis, [(i, (i + 1) % count) for i in range(ends)]),
                cells,
                lax.ppermute(head, axis, [((i + 1) % count, i) for i in range(ends)]),
            ],
            axis=dim,
        )
    return cells


def from_behind(array, axis, by):
    devices = lax.axis_size(axis)
    pairs = [(i, i + by) for i in range(devices) if 0 <= i + by < devices]
    return lax.ppermute(array, axis, pairs)


def sum_squares(values):
    return jnp.sum(jnp.square(values.astype(jnp.float32)), axis=0)


def cross_rows(variant_panel, phenotypes):
    return lax.dot_general(
        variant_panel, phenotypes, (((0,), (0,)), ((), ())), preferred_element_type=jnp.float32
    )


def dense(dosages, phenotypes, window_low, window_high):
    sample_rows, block_width = dosages.shape
    peak_width = phenotypes.shape[1]
    span_width = block_width + 2 * HALO
    samp_count = lax.axis_size("samp")
    samp_index = lax.axis_index("samp")
    pos_index = lax.axis_index("pos")
    share_rows = span_width // samp_count
    own_first = samp_index * share_rows
    near_peaks = padded(phenotypes, (("pos", 1),), peak_width)
    own_tile = cross_rows(dosages, phenotypes)
    lower_edge = cross_rows(dosages[:, :HALO], near_peaks[:, :peak_width])
    upper_edge = cross_rows(dosages[:, block_width - HALO :], near_peaks[:, 2 * peak_width :])
    from_below = from_behind(upper_edge, "pos", 1)
    from_above = from_behind(lower_edge, "pos", -1)
    assembled = jnp.concatenate([from_below, own_tile, from_above], axis=0)
    owned_squares = lax.psum(sum_squares(dosages), "samp")
    peak_total = lax.psum(sum_squares(phenotypes), "samp")
    variant_total = padded(owned_squares, (("pos", 0),), HALO)
    pieces = assembled.reshape(samp_count, share_rows, peak_width)
    cross_share = jnp.sum(lax.all_to_all(pieces, "samp", 0, 0, tiled=True), axis=0)
    variant_share = lax.dynamic_slice_in_dim(variant_total, own_first, share_rows, 0)
    variant_index = (
        pos_index * block_width
        - HALO
        + own_first
        + jnp.arange(share_rows, dtype=jnp.int32)[:, None]
    )
    inside = (variant_index >= window_low[None, :]) & (variant_index <= window_high[None, :])
    factor = math.sqrt(float(sample_rows * samp_count - 2))
    scale_terms = (variant_share[:, None] + EPS) * (peak_total[None, :] + EPS)
    statistic = factor * cross_share / jnp.sqrt(scale_terms)
    return jnp.where(inside, statistic, jnp.zeros_like(statistic))


def squares_by_eight(values):
    wide = jnp.square(values.astype(jnp.float32))
    rows, columns = wide.shape
    return jnp.sum(wide.reshape(rows // EXTRA, EXTRA, columns), axis=0)


def nt(a, b):
    return lax.dot_general(a, b, (((1,), (1,)), ((), ())), preferred_element_type=jnp.float32)


def tn(a, b):
    return lax.dot_general(a, b, (((0,), (0,)), ((), ())), preferred_element_type=jnp.float32)


def nn(a, b):
    return lax.dot_general(a, b, (((1,), (0,)), ((), ())), preferred_element_type=jnp.float32)


def packed_kernel(blocks, factor, d_hbm, p_hbm, low_ref, high_ref, out_ref, most_ref, m, sem):
    d, p, pt, pick, own, vs8 = (m[n] for n in ("d", "p", "pt", "pick", "own", "vs8"))
    samples, variants = d.shape
    peaks = p.shape[1]
    step = samples // STEPS
    quarter = samples // PARTS
    half = variants // 2
    last = len(PIECES) - 1
    s = lax.axis_index("samp")
    b = lax.axis_index("pos")
    x = s // 2
    c = s % 2
    k = x // 2
    r = x % 2
    outer = (x == 0) | (x == 3)
    has_above = b < blocks - 1
    has_below = b > 0
    others = jnp.where(has_above, 1, 0) + jnp.where(has_below, 1, 0)
    above = (b + 1) % blocks
    below = (b + blocks - 1) % blocks
    sibling = {"samp": x * 2 + 1 - c, "pos": b}
    across = {"samp": (3 - x) * 2 + c, "pos": b}
    beside = {"samp": (x + 1 - 2 * (x % 2)) * 2 + c, "pos": b}

    def local(source, target, semaphore, i):
        rows = pl.ds(pl.multiple_of(i * step, step), step)
        return pltpu.make_async_copy(source.at[rows], target.at[rows], semaphore.at[i])

    def send(source, target, name, at, device, arrival=None):
        return pltpu.make_async_remote_copy(
            src_ref=source,
            dst_ref=target,
            send_sem=sem[name + "_send"].at[at],
            recv_sem=sem[name + "_recv"].at[at if arrival is None else arrival],
            device_id=device,
            device_id_type=MESH,
        )

    m["need_in"][0] = jnp.zeros((EXTRA, LANES), jnp.float32)
    barrier = pltpu.get_barrier_semaphore()

    def greet(samp, pos):
        pl.semaphore_signal(
            barrier, inc=1, device_id={"samp": samp, "pos": pos}, device_id_type=MESH
        )

    for i in range(STEPS):
        local(p_hbm, p, sem["p"], i).start()
    for i in range(1, 8):
        greet((s + i) % 8, b)
    for i in range(4):

        @pl.when(s + i > 0)
        def _(i=i):
            greet(s, (b + blocks - 4 * s - i) % blocks)

    @pl.when(has_below)
    def _():
        greet(s, below)

    @pl.when(has_above)
    def _():
        greet(s, above)

    @pl.when((x == 0) & has_below)
    def _():
        for i in range(4):
            greet(2 * i + c, below)

    @pl.when((x == 3) & has_above)
    def _():
        for i in range(4):
            greet(2 * i + c, above)

    first = b * variants
    low = low_ref[...].reshape(1, peaks)
    high = high_ref[...].reshape(1, peaks)
    before = lax.broadcasted_iota(jnp.int32, (peaks, peaks), 0) < lax.broadcasted_iota(
        jnp.int32, (peaks, peaks), 1
    )
    before = jnp.where(before, 1.0, 0.0).astype(jnp.bfloat16)
    slot = lax.broadcasted_iota(jnp.int32, (CAP, peaks), 0).astype(jnp.float32)
    count = jnp.zeros((1, 1), jnp.float32)
    for side, reach in enumerate((low < first, high >= first + variants)):
        flag = jnp.where(reach, 1.0, 0.0)
        rank = nn(jnp.broadcast_to(flag, (16, peaks)).astype(jnp.bfloat16), before)[0:1]
        rank = jnp.where(reach, rank, -1.0)
        count = jnp.maximum(count, jnp.sum(flag, axis=1, keepdims=True))
        pick[side * CAP : (side + 1) * CAP] = jnp.where(slot == rank, 1.0, 0.0).astype(
            jnp.bfloat16
        )
    m["need"][...] = jnp.broadcast_to(count, (EXTRA, LANES))

    def need_copy(i):
        device = {"samp": s, "pos": (b + 4 * s + i) % blocks}
        return send(m["need"], m["need_in"].at[i], "need", i, device)

    def for_each_need(act):
        for i in range(4):

            @pl.when(s + i > 0)
            def _(i=i):
                act(need_copy(i))

    to_side = (has_below, has_above)
    from_side = (has_above, has_below)

    def sel_copy(side, piece, part):
        device = {"samp": s, "pos": (below, above)[side]}
        return send(
            m["out_sel"][piece].at[side, part],
            m["in_sel"][piece].at[side, part],
            "sel",
            (piece, side, part),
            device,
        )

    def select(part, carry):
        for i in range(STEPS // PARTS):
            at = part * (STEPS // PARTS) + i
            local(p_hbm, p, sem["p"], at).wait()
            rows = pl.ds(pl.multiple_of(at * step, step), step)
            got = nt(pick[...], p[rows, :]).astype(jnp.bfloat16)
            for side in range(2):
                top = side * CAP
                for piece, size in enumerate(PIECES):
                    m["out_sel"][piece][side, part, :, i * step : (i + 1) * step] = got[
                        top : top + size
                    ]
                    top += size

        @pl.when(part == 0)
        def _():
            pl.semaphore_wait(barrier, 11 - jnp.where(s == 0, 1, 0) + 2 * others)
            for_each_need(lambda copy: copy.start())

        for side in range(2):

            @pl.when(to_side[side])
            def _(side=side):
                sel_copy(side, 0, part).start()

        return carry

    lax.fori_loop(0, PARTS, select, 0)
    for i in range(STEPS):
        local(d_hbm, d, sem["d"], i).start()
    for piece in range(1, len(PIECES)):
        for part in range(PARTS):
            for side in range(2):

                @pl.when(to_side[side])
                def _(piece=piece, part=part, side=side):
                    sel_copy(side, piece, part).start()

    same = lax.broadcasted_iota(jnp.int32, (peaks, peaks), 0) == lax.broadcasted_iota(
        jnp.int32, (peaks, peaks), 1
    )
    same = jnp.where(same, 1.0, 0.0).astype(jnp.bfloat16)

    def turn(i, total):
        rows = pl.ds(pl.multiple_of(i * step, step), step)
        part = p[rows, :]
        pt[:, rows] = nt(same, part).astype(jnp.bfloat16)
        return total + squares_by_eight(part)

    slots = m["ps_slots"]
    slots[s, :, 0:peaks] = lax.fori_loop(
        0, STEPS, turn, jnp.zeros((EXTRA, peaks), jnp.float32)
    )

    def ps_copy(i):
        device = {"samp": (s + i) % 8, "pos": b}
        return send(slots.at[s], slots.at[s], "ps", i, device, s)

    own[...] = jnp.zeros_like(own)
    vs8[...] = jnp.zeros_like(vs8)

    def multiply(i, carry):
        local(d_hbm, d, sem["d"], i).wait()
        rows = pl.ds(pl.multiple_of(i * step, step), step)
        part = pt[:, rows]
        for q in range(4):
            columns = slice(q * QUARTER, (q + 1) * QUARTER)
            own[q % 2, q // 2, 0:peaks, :] += nn(part, d[rows, columns])
        vs8[...] += squares_by_eight(d[rows, :])
        return carry

    lax.fori_loop(0, STEPS, multiply, 0)
    for q in range(4):
        own[q % 2, q // 2, peaks : peaks + EXTRA, :] = vs8[:, q * QUARTER : (q + 1) * QUARTER]

    tall = peaks + EXTRA
    cuts = [pl.ds(0, 192), pl.ds(192, tall - 192)]
    own0, own1, own2 = m["own0"], m["own1"], m["own2"]

    def own_a(j):
        return send(own.at[1 - c, :, cuts[j]], own0.at[:, cuts[j]], "own", (0, j), sibling)

    def own_b(j):
        return send(own0.at[1 - k, cuts[j]], own1.at[cuts[j]], "own", (1, j), across)

    def own_c(j):
        return send(own1.at[cuts[j]], own2.at[cuts[j]], "own", (2, j), beside)

    def own_by_core(j):
        own_a(j).wait_recv()
        own0[:, cuts[j], :] = own0[:, cuts[j], :] + own[c, :, cuts[j], :]
        own_b(j).start()

    def own_by_chip(j):
        own_b(j).wait_recv()
        own1[cuts[j], :] = own1[cuts[j], :] + own0[k, cuts[j], :]

        @pl.when(outer)
        def _():
            own_c(j).start()

    edge, edge0, edge1, edge2, edge3 = (m[n] for n in ("edge", "edge0", "edge1", "edge2", "edge3"))

    def e0(piece):
        return send(edge[piece].at[1 - c], edge0[piece], "e0", piece, sibling)

    def e1(piece):
        return send(edge0[piece].at[1 - k], edge1[piece], "e1", piece, across)

    def rows_of(piece, which):
        size = PIECES[piece] + EXTRA
        share = edge2[piece].shape[0]
        return pl.ds(pl.multiple_of(which * (size - share), EXTRA), share)

    def e2(piece):
        return send(edge1[piece].at[rows_of(piece, 1 - r)], edge2[piece], "e2", piece, beside)

    def e3(piece):
        device = {"samp": 6 * k + c, "pos": (b + blocks + 1 - 2 * k) % blocks}
        return send(edge2[piece], edge3[piece].at[r], "e3", piece, device, (piece, r))

    def e3_from(piece, which):
        return send(
            edge2[piece], edge3[piece].at[which], "e3", piece, sibling, (piece, which)
        )

    returns = jnp.where(k == 0, has_above, has_below)

    def straight(side):
        device = {"samp": 6 * side + c, "pos": (above, below)[side]}
        return send(edge0[last].at[side], m["ends"].at[x], "ends", side, device, x)

    def edges(piece, parts):
        size = PIECES[piece]

        def part(i, carry):
            rows = pl.ds(pl.multiple_of(i * quarter, quarter), quarter)
            for side in range(2):


                @pl.when(from_side[side])
                def _(side=side):
                    sel_copy(side, piece, i).wait_recv()
                    base = half * (1 - side)
                    got = nn(m["in_sel"][piece][side, i], d[rows, base : base + half])
                    for core in range(2):
                        edge[piece][core, side, 0:size, :] += got[
                            :, core * QUARTER : (core + 1) * QUARTER
                        ]

            return carry

        lax.fori_loop(parts[0], parts[1], part, 0)

    def clear(piece):
        edge[piece][...] = jnp.zeros_like(edge[piece])

    def edges_by_core(piece):
        e0(piece).wait_recv()
        edge0[piece][...] = edge0[piece][...] + edge[piece][c]
        if piece == last:
            for side in range(2):

                @pl.when(from_side[side])
                def _(side=side):
                    straight(side).start()

        else:
            e1(piece).start()

    def edges_by_chip(piece):
        e1(piece).wait_recv()
        edge1[piece][...] = edge1[piece][...] + edge0[piece][k]
        e2(piece).start()

    def edges_by_half(piece):
        e2(piece).wait_recv()
        edge2[piece][...] = edge2[piece][...] + edge1[piece][rows_of(piece, r), :]

        @pl.when(returns)
        def _():
            e3(piece).start()

    for j in range(2):
        own_a(j).start()
    for piece in range(len(PIECES)):
        clear(piece)
    for side in range(2):
        base = half * (1 - side)
        for core in range(2):
            edge[0][core, side, PIECES[0] :, :] = vs8[
                :, base + core * QUARTER : base + (core + 1) * QUARTER
            ]
    for_each_need(lambda copy: copy.wait_recv())
    worst = m["need"][...]
    for i in range(4):
        worst = jnp.maximum(worst, m["need_in"][i])
    slots[s, :, peaks:] = worst
    for i in range(1, 8):
        ps_copy(i).start()
    own_by_core(0)
    own_by_core(1)
    edges(0, (0, PARTS))
    e0(0).start()
    own_by_chip(0)
    edges_by_core(0)

    for i in range(1, 8):
        sender = (s + i) % 8
        send(slots.at[sender], slots.at[sender], "ps", i, sibling, sender).wait_recv()
    ps = slots[0, :, 0:peaks]
    worst = slots[0, :, peaks:]
    for i in range(1, 8):
        ps = ps + slots[i, :, 0:peaks]
        worst = jnp.maximum(worst, slots[i, :, peaks:])
    most_ref[0] = jnp.max(worst)
    peak_scale = factor / jnp.sqrt(jnp.sum(ps, axis=0, keepdims=True) + EPS)

    own_by_chip(1)
    edges_by_chip(0)
    edges(1, (0, 2))
    edges_by_half(0)
    edges(1, (2, PARTS))
    e0(1).start()
    edges_by_core(1)

    def finish(cross):
        index = (
            first
            - HALO
            + s * QUARTER
            + lax.broadcasted_iota(jnp.int32, (QUARTER, peaks), 0)
        )
        inside = (index >= low) & (index <= high)
        out_ref[...] = jnp.where(inside, cross * peak_scale, 0.0)

    def variant_scale(eight):
        return 1.0 / jnp.sqrt(jnp.sum(eight, axis=0, keepdims=True) + EPS)

    @pl.when(jnp.logical_not(outer))
    def _():
        for j in range(2):
            own_c(j).wait_recv()
        scale = variant_scale(own1[peaks:tall] + own2[peaks:tall])
        finish(((own1[0:peaks] + own2[0:peaks]) * scale).T)

    @pl.when(outer)
    def _():
        for j in range(2):
            own_c(j).wait_send()

    for side in range(2):

        @pl.when((x == 3 * side) & to_side[side])
        def _(side=side):
            for which in range(2):
                e3_from(0, which).wait_recv()
            share = edge3[0].shape[1]
            size = PIECES[0]
            scale = variant_scale(edge3[0][1, share - EXTRA :])
            cross = jnp.zeros((QUARTER, peaks), jnp.float32)

            def placed(cross, rest, top):
                rest = rest * scale
                chosen = pick[top : top + rest.shape[0]]
                for _ in range(3):
                    upper = rest.astype(jnp.bfloat16)
                    cross = cross + tn(upper, chosen)
                    rest = rest - upper.astype(jnp.float32)
                return cross

            joined = m["joined"]
            joined[0:share] = edge3[0][0]
            joined[share:size] = edge3[0][1, 2 * share - size - EXTRA : share - EXTRA]
            cross = placed(cross, joined[...], side * CAP)
            for i in range(4):
                send(
                    edge0[last].at[side], m["ends"].at[i], "ends", side, sibling, i
                ).wait_recv()
            rest = m["ends"][0] + m["ends"][1] + m["ends"][2] + m["ends"][3]
            finish(placed(cross, rest, side * CAP + size))

        @pl.when((x == 3 * side) & jnp.logical_not(to_side[side]))
        def _():
            out_ref[...] = jnp.zeros((QUARTER, peaks), jnp.float32)

    def sent(part, carry):
        for side in range(2):

            @pl.when(to_side[side])
            def _(side=side):
                for piece in range(len(PIECES)):
                    sel_copy(side, piece, part).wait_send()

        return carry

    lax.fori_loop(0, PARTS, sent, 0)
    for piece in range(len(PIECES)):
        e0(piece).wait_send()
    e1(0).wait_send()
    e2(0).wait_send()

    @pl.when(returns)
    def _():
        e3(0).wait_send()

    for side in range(2):

        @pl.when(from_side[side])
        def _(side=side):
            straight(side).wait_send()

    for i in range(1, 8):
        ps_copy(i).wait_send()
    for_each_need(lambda copy: copy.wait_send())
    for j in range(2):
        own_a(j).wait_send()
        own_b(j).wait_send()


def packed_form(dosages, phenotypes, window_low, window_high):
    samples, variants = dosages.shape
    peaks = phenotypes.shape[1]
    samp_count = lax.axis_size("samp")
    factor = math.sqrt(float(samples * samp_count - 2))
    tall = peaks + EXTRA
    f32, bf16 = jnp.float32, jnp.bfloat16
    last = len(PIECES) - 1
    sizes = [size + (EXTRA if i == 0 else 0) for i, size in enumerate(PIECES)]
    memory = {
        "d": ((samples, variants), bf16),
        "p": ((samples, peaks), bf16),
        "pt": ((peaks, samples), bf16),
        "pick": ((2 * CAP, peaks), bf16),
        "own": ((2, 2, tall, QUARTER), f32),
        "own0": ((2, tall, QUARTER), f32),
        "own1": ((tall, QUARTER), f32),
        "own2": ((tall, QUARTER), f32),
        "vs8": ((EXTRA, variants), f32),
        "ps_slots": ((8, EXTRA, peaks + LANES), f32),
        "need": ((EXTRA, LANES), f32),
        "need_in": ((4, EXTRA, LANES), f32),
        "joined": ((PIECES[0], QUARTER), f32),
        "ends": ((4, PIECES[last], QUARTER), f32),
    }
    memory = {name: pltpu.VMEM(*of) for name, of in memory.items()}
    for name in ("out_sel", "in_sel"):
        memory[name] = [
            pltpu.VMEM((2, PARTS, size, samples // PARTS), bf16) for size in PIECES
        ]
    memory["edge"] = [pltpu.VMEM((2, 2, size, QUARTER), f32) for size in sizes]
    memory["edge0"] = [pltpu.VMEM((2, size, QUARTER), f32) for size in sizes]
    memory["edge1"] = [pltpu.VMEM((size, QUARTER), f32) for size in sizes[:last]]
    shares = [-(-size // (2 * EXTRA)) * EXTRA for size in sizes[:last]]
    memory["edge2"] = [pltpu.VMEM((share, QUARTER), f32) for share in shares]
    memory["edge3"] = [pltpu.VMEM((2, share, QUARTER), f32) for share in shares]
    dma = pltpu.SemaphoreType.DMA
    semaphores = {"p": dma((STEPS,)), "d": dma((STEPS,))}
    for name, shape in (
        ("sel", (len(PIECES), 2, PARTS)),
        ("need", (4,)),
        ("ps", (8,)),
        ("own", (3, 2)),
        ("e0", (len(PIECES),)),
        ("e1", (last,)),
        ("e2", (last,)),
    ):
        semaphores[name + "_send"] = dma(shape)
        semaphores[name + "_recv"] = dma(shape)
    semaphores["e3_send"] = dma((last,))
    semaphores["e3_recv"] = dma((last, 2))
    semaphores["ends_send"] = dma((2,))
    semaphores["ends_recv"] = dma((4,))
    return pl.pallas_call(
        functools.partial(packed_kernel, lax.axis_size("pos"), factor),
        out_shape=(
            jax.ShapeDtypeStruct((QUARTER, peaks), f32),
            jax.ShapeDtypeStruct((1,), f32),
        ),
        in_specs=[pl.BlockSpec(memory_space=pl.ANY)] * 2
        + [pl.BlockSpec(memory_space=pltpu.VMEM)] * 2,
        out_specs=(
            pl.BlockSpec(memory_space=pltpu.VMEM),
            pl.BlockSpec(memory_space=pltpu.SMEM),
        ),
        scratch_shapes=[memory, semaphores],
        compiler_params=pltpu.CompilerParams(
            collective_id=0, has_side_effects=True, vmem_limit_bytes=63 << 20
        ),
    )(dosages, phenotypes, window_low, window_high)


def shards(dosages, phenotypes, window_low, window_high):
    found, most = packed_form(dosages, phenotypes, window_low, window_high)
    found = lax.cond(
        most[0] > CAP,
        lambda: dense(dosages, phenotypes, window_low, window_high),
        lambda: found,
    )
    return found[None]


def solution(mesh):
    placed = (P("samp", "pos"), P("samp", "pos"), P("pos"), P("pos"))
    return jax.shard_map(
        shards, mesh=mesh, in_specs=placed, out_specs=P("pos", "samp", None), check_vma=False
    )
```

```python
import functools
import math

import jax
import jax.numpy as jnp
from jax import lax
from jax.experimental import pallas as pl
from jax.experimental.pallas import tpu as pltpu
from jax.sharding import PartitionSpec as P

HALO = 512
EPS = 1e-06
MESH = pl.DeviceIdType.MESH

PIECES = (96, 48)
CAP = sum(PIECES)
QUARTER = 256
EXTRA = 8
LANES = 128
STEPS = 8
PARTS = 4


def padded(cells, sides, width):
    for axis, dim in sides:
        count = lax.axis_size(axis)
        ends = count - 1
        head = lax.slice_in_dim(cells, 0, width, axis=dim)
        tail = lax.slice_in_dim(cells, cells.shape[dim] - width, cells.shape[dim], axis=dim)
        cells = jnp.concatenate(
            [
                lax.ppermute(tail, axis, [(i, (i + 1) % count) for i in range(ends)]),
                cells,
                lax.ppermute(head, axis, [((i + 1) % count, i) for i in range(ends)]),
            ],
            axis=dim,
        )
    return cells


def from_behind(array, axis, by):
    devices = lax.axis_size(axis)
    pairs = [(i, i + by) for i in range(devices) if 0 <= i + by < devices]
    return lax.ppermute(array, axis, pairs)


def sum_squares(values):
    return jnp.sum(jnp.square(values.astype(jnp.float32)), axis=0)


def cross_rows(variant_panel, phenotypes):
    return lax.dot_general(
        variant_panel, phenotypes, (((0,), (0,)), ((), ())), preferred_element_type=jnp.float32
    )


def dense(dosages, phenotypes, window_low, window_high):
    sample_rows, block_width = dosages.shape
    peak_width = phenotypes.shape[1]
    span_width = block_width + 2 * HALO
    samp_count = lax.axis_size("samp")
    samp_index = lax.axis_index("samp")
    pos_index = lax.axis_index("pos")
    share_rows = span_width // samp_count
    own_first = samp_index * share_rows
    near_peaks = padded(phenotypes, (("pos", 1),), peak_width)
    own_tile = cross_rows(dosages, phenotypes)
    lower_edge = cross_rows(dosages[:, :HALO], near_peaks[:, :peak_width])
    upper_edge = cross_rows(dosages[:, block_width - HALO :], near_peaks[:, 2 * peak_width :])
    from_below = from_behind(upper_edge, "pos", 1)
    from_above = from_behind(lower_edge, "pos", -1)
    assembled = jnp.concatenate([from_below, own_tile, from_above], axis=0)
    owned_squares = lax.psum(sum_squares(dosages), "samp")
    peak_total = lax.psum(sum_squares(phenotypes), "samp")
    variant_total = padded(owned_squares, (("pos", 0),), HALO)
    pieces = assembled.reshape(samp_count, share_rows, peak_width)
    cross_share = jnp.sum(lax.all_to_all(pieces, "samp", 0, 0, tiled=True), axis=0)
    variant_share = lax.dynamic_slice_in_dim(variant_total, own_first, share_rows, 0)
    variant_index = (
        pos_index * block_width
        - HALO
        + own_first
        + jnp.arange(share_rows, dtype=jnp.int32)[:, None]
    )
    inside = (variant_index >= window_low[None, :]) & (variant_index <= window_high[None, :])
    factor = math.sqrt(float(sample_rows * samp_count - 2))
    scale_terms = (variant_share[:, None] + EPS) * (peak_total[None, :] + EPS)
    statistic = factor * cross_share / jnp.sqrt(scale_terms)
    return jnp.where(inside, statistic, jnp.zeros_like(statistic))


def squares_by_eight(values):
    wide = jnp.square(values.astype(jnp.float32))
    rows, columns = wide.shape
    return jnp.sum(wide.reshape(rows // EXTRA, EXTRA, columns), axis=0)


def nt(a, b):
    return lax.dot_general(a, b, (((1,), (1,)), ((), ())), preferred_element_type=jnp.float32)


def tn(a, b):
    return lax.dot_general(a, b, (((0,), (0,)), ((), ())), preferred_element_type=jnp.float32)


def nn(a, b):
    return lax.dot_general(a, b, (((1,), (0,)), ((), ())), preferred_element_type=jnp.float32)


def packed_kernel(blocks, factor, d_hbm, p_hbm, low_ref, high_ref, out_ref, most_ref, m, sem):
    d, p, pt, pick, own, vs8 = (m[n] for n in ("d", "p", "pt", "pick", "own", "vs8"))
    samples, variants = d.shape
    peaks = p.shape[1]
    step = samples // STEPS
    quarter = samples // PARTS
    half = variants // 2
    last = len(PIECES) - 1
    s = lax.axis_index("samp")
    b = lax.axis_index("pos")
    x = s // 2
    c = s % 2
    k = x // 2
    r = x % 2
    outer = (x == 0) | (x == 3)
    has_above = b < blocks - 1
    has_below = b > 0
    root = b == 0
    teller = (s == b // 4) & (b > 0)
    others = jnp.where(has_above, 1, 0) + jnp.where(has_below, 1, 0)
    above = (b + 1) % blocks
    below = (b + blocks - 1) % blocks
    sibling = {"samp": x * 2 + 1 - c, "pos": b}
    across = {"samp": (3 - x) * 2 + c, "pos": b}
    beside = {"samp": (x + 1 - 2 * (x % 2)) * 2 + c, "pos": b}

    def local(source, target, semaphore, i):
        rows = pl.ds(pl.multiple_of(i * step, step), step)
        return pltpu.make_async_copy(source.at[rows], target.at[rows], semaphore.at[i])

    def send(source, target, name, at, device, arrival=None):
        return pltpu.make_async_remote_copy(
            src_ref=source,
            dst_ref=target,
            send_sem=sem[name + "_send"].at[at],
            recv_sem=sem[name + "_recv"].at[at if arrival is None else arrival],
            device_id=device,
            device_id_type=MESH,
        )

    m["need_in"][...] = jnp.zeros_like(m["need_in"])
    barrier = pltpu.get_barrier_semaphore()

    def greet(samp, pos):
        pl.semaphore_signal(
            barrier, inc=1, device_id={"samp": samp, "pos": pos}, device_id_type=MESH
        )

    for i in range(STEPS):
        local(p_hbm, p, sem["p"], i).start()
    for i in range(1, 8):
        greet((s + i) % 8, b)
    @pl.when(root)
    def _():
        for i in range(4):

            @pl.when(s + i > 0)
            def _(i=i):
                greet(s, 4 * s + i)

    @pl.when(has_below)
    def _():
        greet(s, below)

    @pl.when(has_above)
    def _():
        greet(s, above)

    @pl.when((x == 0) & has_below)
    def _():
        for i in range(4):
            greet(2 * i + c, below)

    @pl.when((x == 3) & has_above)
    def _():
        for i in range(4):
            greet(2 * i + c, above)

    first = b * variants
    low = low_ref[...].reshape(1, peaks)
    high = high_ref[...].reshape(1, peaks)
    before = lax.broadcasted_iota(jnp.int32, (peaks, peaks), 0) < lax.broadcasted_iota(
        jnp.int32, (peaks, peaks), 1
    )
    before = jnp.where(before, 1.0, 0.0).astype(jnp.bfloat16)
    slot = lax.broadcasted_iota(jnp.int32, (CAP, peaks), 0).astype(jnp.float32)
    count = jnp.zeros((1, 1), jnp.float32)
    for side, reach in enumerate((low < first, high >= first + variants)):
        flag = jnp.where(reach, 1.0, 0.0)
        rank = nn(jnp.broadcast_to(flag, (16, peaks)).astype(jnp.bfloat16), before)[0:1]
        rank = jnp.where(reach, rank, -1.0)
        count = jnp.maximum(count, jnp.sum(flag, axis=1, keepdims=True))
        pick[side * CAP : (side + 1) * CAP] = jnp.where(slot == rank, 1.0, 0.0).astype(
            jnp.bfloat16
        )
    m["need"][...] = jnp.broadcast_to(count, (EXTRA, LANES))

    told = m["told"]

    def tell():
        return send(m["need"], m["need_in"].at[b % 4], "need", b % 4, {"samp": s, "pos": 0})

    def heard(i):
        return send(m["need"], m["need_in"].at[i], "need", i, sibling)

    def answer(i):
        return send(m["need"], told, "answer", i, {"samp": s, "pos": 4 * s + i}, 0)

    def answer_here():
        return send(m["need"], told, "answer", 0, sibling)

    def share(i):
        return send(told, told, "share", i, {"samp": (s + i) % 8, "pos": b}, 0)

    def for_each_heard(act):
        for i in range(4):

            @pl.when(root & (s + i > 0))
            def _(i=i):
                act(i)

    to_side = (has_below, has_above)
    from_side = (has_above, has_below)

    def sel_copy(side, piece, part):
        device = {"samp": s, "pos": (below, above)[side]}
        return send(
            m["out_sel"][piece].at[side, part],
            m["in_sel"][piece].at[side, part],
            "sel",
            (piece, side, part),
            device,
        )

    def select(part, carry):
        for i in range(STEPS // PARTS):
            at = part * (STEPS // PARTS) + i
            local(p_hbm, p, sem["p"], at).wait()
            rows = pl.ds(pl.multiple_of(at * step, step), step)
            got = nt(pick[...], p[rows, :]).astype(jnp.bfloat16)
            for side in range(2):
                top = side * CAP
                for piece, size in enumerate(PIECES):
                    m["out_sel"][piece][side, part, :, i * step : (i + 1) * step] = got[
                        top : top + size
                    ]
                    top += size

        @pl.when(part == 0)
        def _():
            pl.semaphore_wait(barrier, 7 + 2 * others + jnp.where(teller, 1, 0))

            @pl.when(teller)
            def _():
                tell().start()

        for side in range(2):

            @pl.when(to_side[side])
            def _(side=side):
                sel_copy(side, 0, part).start()

        return carry

    lax.fori_loop(0, PARTS, select, 0)
    for i in range(STEPS):
        local(d_hbm, d, sem["d"], i).start()
    for piece in range(1, len(PIECES)):
        for part in range(PARTS):
            for side in range(2):

                @pl.when(to_side[side])
                def _(piece=piece, part=part, side=side):
                    sel_copy(side, piece, part).start()

    same = lax.broadcasted_iota(jnp.int32, (peaks, peaks), 0) == lax.broadcasted_iota(
        jnp.int32, (peaks, peaks), 1
    )
    same = jnp.where(same, 1.0, 0.0).astype(jnp.bfloat16)

    def turn(i, total):
        rows = pl.ds(pl.multiple_of(i * step, step), step)
        part = p[rows, :]
        pt[:, rows] = nt(same, part).astype(jnp.bfloat16)
        return total + squares_by_eight(part)

    slots = m["ps_slots"]
    slots[s, :, 0:peaks] = lax.fori_loop(
        0, STEPS, turn, jnp.zeros((EXTRA, peaks), jnp.float32)
    )

    def ps_copy(i):
        device = {"samp": (s + i) % 8, "pos": b}
        return send(slots.at[s], slots.at[s], "ps", i, device, s)

    own[...] = jnp.zeros_like(own)
    vs8[...] = jnp.zeros_like(vs8)

    def multiply(i, carry):
        local(d_hbm, d, sem["d"], i).wait()
        rows = pl.ds(pl.multiple_of(i * step, step), step)
        part = pt[:, rows]
        for q in range(4):
            columns = slice(q * QUARTER, (q + 1) * QUARTER)
            own[q % 2, q // 2, 0:peaks, :] += nn(part, d[rows, columns])
        vs8[...] += squares_by_eight(d[rows, :])
        return carry

    lax.fori_loop(0, STEPS, multiply, 0)
    for q in range(4):
        own[q % 2, q // 2, peaks : peaks + EXTRA, :] = vs8[:, q * QUARTER : (q + 1) * QUARTER]

    tall = peaks + EXTRA
    cuts = [pl.ds(0, 192), pl.ds(192, tall - 192)]
    own0, own1, own2 = m["own0"], m["own1"], m["own2"]

    def own_a(j):
        return send(own.at[1 - c, :, cuts[j]], own0.at[:, cuts[j]], "own", (0, j), sibling)

    def own_b(j):
        return send(own0.at[1 - k, cuts[j]], own1.at[cuts[j]], "own", (1, j), across)

    def own_c(j):
        return send(own1.at[cuts[j]], own2.at[cuts[j]], "own", (2, j), beside)

    def own_by_core(j):
        own_a(j).wait_recv()
        own0[:, cuts[j], :] = own0[:, cuts[j], :] + own[c, :, cuts[j], :]
        own_b(j).start()

    def own_by_chip(j):
        own_b(j).wait_recv()
        own1[cuts[j], :] = own1[cuts[j], :] + own0[k, cuts[j], :]

        @pl.when(outer)
        def _():
            own_c(j).start()

    edge, edge0, edge1, edge2, edge3 = (m[n] for n in ("edge", "edge0", "edge1", "edge2", "edge3"))

    def e0(piece):
        return send(edge[piece].at[1 - c], edge0[piece], "e0", piece, sibling)

    def e1(piece):
        return send(edge0[piece].at[1 - k], edge1[piece], "e1", piece, across)

    def rows_of(piece, which):
        size = PIECES[piece] + EXTRA
        share = edge2[piece].shape[0]
        return pl.ds(pl.multiple_of(which * (size - share), EXTRA), share)

    def e2(piece):
        return send(edge1[piece].at[rows_of(piece, 1 - r)], edge2[piece], "e2", piece, beside)

    def e3(piece):
        device = {"samp": 6 * k + c, "pos": (b + blocks + 1 - 2 * k) % blocks}
        return send(edge2[piece], edge3[piece].at[r], "e3", piece, device, (piece, r))

    def e3_from(piece, which):
        return send(
            edge2[piece], edge3[piece].at[which], "e3", piece, sibling, (piece, which)
        )

    returns = jnp.where(k == 0, has_above, has_below)

    def straight(side):
        device = {"samp": 6 * side + c, "pos": (above, below)[side]}
        return send(edge0[last].at[side], m["ends"].at[x], "ends", side, device, x)

    def edges(piece, parts):
        size = PIECES[piece]

        def part(i, carry):
            rows = pl.ds(pl.multiple_of(i * quarter, quarter), quarter)
            for side in range(2):


                @pl.when(from_side[side])
                def _(side=side):
                    sel_copy(side, piece, i).wait_recv()
                    base = half * (1 - side)
                    got = nn(m["in_sel"][piece][side, i], d[rows, base : base + half])
                    for core in range(2):
                        edge[piece][core, side, 0:size, :] += got[
                            :, core * QUARTER : (core + 1) * QUARTER
                        ]

            return carry

        lax.fori_loop(parts[0], parts[1], part, 0)

    def clear(piece):
        edge[piece][...] = jnp.zeros_like(edge[piece])

    def edges_by_core(piece):
        e0(piece).wait_recv()
        edge0[piece][...] = edge0[piece][...] + edge[piece][c]
        if piece == last:
            for side in range(2):

                @pl.when(from_side[side])
                def _(side=side):
                    straight(side).start()

        else:
            e1(piece).start()

    def edges_by_chip(piece):
        e1(piece).wait_recv()
        edge1[piece][...] = edge1[piece][...] + edge0[piece][k]
        e2(piece).start()

    def edges_by_half(piece):
        e2(piece).wait_recv()
        edge2[piece][...] = edge2[piece][...] + edge1[piece][rows_of(piece, r), :]

        @pl.when(returns)
        def _():
            e3(piece).start()

    for j in range(2):
        own_a(j).start()
    for piece in range(len(PIECES)):
        clear(piece)
    for side in range(2):
        base = half * (1 - side)
        for core in range(2):
            edge[0][core, side, PIECES[0] :, :] = vs8[
                :, base + core * QUARTER : base + (core + 1) * QUARTER
            ]
    for_each_heard(lambda i: heard(i).wait_recv())
    worst = m["need"][...]
    for i in range(4):
        worst = jnp.maximum(worst, m["need_in"][i])
    slots[s, :, peaks:] = worst
    for i in range(1, 8):
        ps_copy(i).start()
    own_by_core(0)
    own_by_core(1)
    edges(0, (0, 2))
    own_by_chip(0)
    edges(0, (2, 3))
    own_by_chip(1)
    edges(0, (3, PARTS))
    e0(0).start()

    for i in range(1, 8):
        sender = (s + i) % 8
        send(slots.at[sender], slots.at[sender], "ps", i, sibling, sender).wait_recv()
    ps = slots[0, :, 0:peaks]
    worst = slots[0, :, peaks:]
    for i in range(1, 8):
        ps = ps + slots[i, :, 0:peaks]
        worst = jnp.maximum(worst, slots[i, :, peaks:])

    @pl.when(teller)
    def _():
        tell().wait_send()

    m["need"][...] = worst
    for_each_heard(lambda i: answer(i).start())
    peak_scale = factor / jnp.sqrt(jnp.sum(ps, axis=0, keepdims=True) + EPS)

    edges_by_core(0)
    edges(1, (0, 2))
    edges_by_chip(0)

    def finish(cross):
        index = (
            first
            - HALO
            + s * QUARTER
            + lax.broadcasted_iota(jnp.int32, (QUARTER, peaks), 0)
        )
        inside = (index >= low) & (index <= high)
        out_ref[...] = jnp.where(inside, cross * peak_scale, 0.0)

    def variant_scale(eight):
        return 1.0 / jnp.sqrt(jnp.sum(eight, axis=0, keepdims=True) + EPS)

    @pl.when(jnp.logical_not(outer))
    def _():
        for j in range(2):
            own_c(j).wait_recv()
        scale = variant_scale(own1[peaks:tall] + own2[peaks:tall])
        finish(((own1[0:peaks] + own2[0:peaks]) * scale).T)

    edges(1, (2, PARTS))
    e0(1).start()
    edges_by_half(0)
    edges_by_core(1)

    @pl.when(teller)
    def _():
        answer_here().wait_recv()
        for i in range(1, 8):
            share(i).start()

    @pl.when(outer)
    def _():
        for j in range(2):
            own_c(j).wait_send()

    for side in range(2):

        @pl.when((x == 3 * side) & to_side[side])
        def _(side=side):
            for which in range(2):
                e3_from(0, which).wait_recv()
            share = edge3[0].shape[1]
            size = PIECES[0]
            scale = variant_scale(edge3[0][1, share - EXTRA :])
            cross = jnp.zeros((QUARTER, peaks), jnp.float32)

            def placed(cross, rest, top):
                rest = rest * scale
                chosen = pick[top : top + rest.shape[0]]
                for _ in range(3):
                    upper = rest.astype(jnp.bfloat16)
                    cross = cross + tn(upper, chosen)
                    rest = rest - upper.astype(jnp.float32)
                return cross

            joined = m["joined"]
            joined[0:share] = edge3[0][0]
            joined[share:size] = edge3[0][1, 2 * share - size - EXTRA : share - EXTRA]
            cross = placed(cross, joined[...], side * CAP)
            for i in range(4):
                send(
                    edge0[last].at[side], m["ends"].at[i], "ends", side, sibling, i
                ).wait_recv()
            rest = m["ends"][0] + m["ends"][1] + m["ends"][2] + m["ends"][3]
            finish(placed(cross, rest, side * CAP + size))

        @pl.when((x == 3 * side) & jnp.logical_not(to_side[side]))
        def _():
            out_ref[...] = jnp.zeros((QUARTER, peaks), jnp.float32)

    @pl.when(root)
    def _():
        most_ref[0] = jnp.max(m["need"][...])

    @pl.when(jnp.logical_not(root | teller))
    def _():
        send(told, told, "share", 1, sibling, 0).wait_recv()

    @pl.when(jnp.logical_not(root))
    def _():
        most_ref[0] = jnp.max(told[...])

    def sent(part, carry):
        for side in range(2):

            @pl.when(to_side[side])
            def _(side=side):
                for piece in range(len(PIECES)):
                    sel_copy(side, piece, part).wait_send()

        return carry

    lax.fori_loop(0, PARTS, sent, 0)
    for piece in range(len(PIECES)):
        e0(piece).wait_send()
    e1(0).wait_send()
    e2(0).wait_send()

    @pl.when(returns)
    def _():
        e3(0).wait_send()

    for side in range(2):

        @pl.when(from_side[side])
        def _(side=side):
            straight(side).wait_send()

    for i in range(1, 8):
        ps_copy(i).wait_send()
    for_each_heard(lambda i: answer(i).wait_send())

    @pl.when(teller)
    def _():
        for i in range(1, 8):
            share(i).wait_send()

    for j in range(2):
        own_a(j).wait_send()
        own_b(j).wait_send()


def packed_form(dosages, phenotypes, window_low, window_high):
    samples, variants = dosages.shape
    peaks = phenotypes.shape[1]
    samp_count = lax.axis_size("samp")
    factor = math.sqrt(float(samples * samp_count - 2))
    tall = peaks + EXTRA
    f32, bf16 = jnp.float32, jnp.bfloat16
    last = len(PIECES) - 1
    sizes = [size + (EXTRA if i == 0 else 0) for i, size in enumerate(PIECES)]
    memory = {
        "d": ((samples, variants), bf16),
        "p": ((samples, peaks), bf16),
        "pt": ((peaks, samples), bf16),
        "pick": ((2 * CAP, peaks), bf16),
        "own": ((2, 2, tall, QUARTER), f32),
        "own0": ((2, tall, QUARTER), f32),
        "own1": ((tall, QUARTER), f32),
        "own2": ((tall, QUARTER), f32),
        "vs8": ((EXTRA, variants), f32),
        "ps_slots": ((8, EXTRA, peaks + LANES), f32),
        "need": ((EXTRA, LANES), f32),
        "told": ((EXTRA, LANES), f32),
        "need_in": ((4, EXTRA, LANES), f32),
        "joined": ((PIECES[0], QUARTER), f32),
        "ends": ((4, PIECES[last], QUARTER), f32),
    }
    memory = {name: pltpu.VMEM(*of) for name, of in memory.items()}
    for name in ("out_sel", "in_sel"):
        memory[name] = [
            pltpu.VMEM((2, PARTS, size, samples // PARTS), bf16) for size in PIECES
        ]
    memory["edge"] = [pltpu.VMEM((2, 2, size, QUARTER), f32) for size in sizes]
    memory["edge0"] = [pltpu.VMEM((2, size, QUARTER), f32) for size in sizes]
    memory["edge1"] = [pltpu.VMEM((size, QUARTER), f32) for size in sizes[:last]]
    shares = [-(-size // (2 * EXTRA)) * EXTRA for size in sizes[:last]]
    memory["edge2"] = [pltpu.VMEM((share, QUARTER), f32) for share in shares]
    memory["edge3"] = [pltpu.VMEM((2, share, QUARTER), f32) for share in shares]
    dma = pltpu.SemaphoreType.DMA
    semaphores = {"p": dma((STEPS,)), "d": dma((STEPS,))}
    for name, shape in (
        ("sel", (len(PIECES), 2, PARTS)),
        ("need", (4,)),
        ("ps", (8,)),
        ("own", (3, 2)),
        ("e0", (len(PIECES),)),
        ("e1", (last,)),
        ("e2", (last,)),
    ):
        semaphores[name + "_send"] = dma(shape)
        semaphores[name + "_recv"] = dma(shape)
    semaphores["answer_send"] = dma((4,))
    semaphores["answer_recv"] = dma((1,))
    semaphores["share_send"] = dma((8,))
    semaphores["share_recv"] = dma((1,))
    semaphores["e3_send"] = dma((last,))
    semaphores["e3_recv"] = dma((last, 2))
    semaphores["ends_send"] = dma((2,))
    semaphores["ends_recv"] = dma((4,))
    return pl.pallas_call(
        functools.partial(packed_kernel, lax.axis_size("pos"), factor),
        out_shape=(
            jax.ShapeDtypeStruct((QUARTER, peaks), f32),
            jax.ShapeDtypeStruct((1,), f32),
        ),
        in_specs=[pl.BlockSpec(memory_space=pl.ANY)] * 2
        + [pl.BlockSpec(memory_space=pltpu.VMEM)] * 2,
        out_specs=(
            pl.BlockSpec(memory_space=pltpu.VMEM),
            pl.BlockSpec(memory_space=pltpu.SMEM),
        ),
        scratch_shapes=[memory, semaphores],
        compiler_params=pltpu.CompilerParams(
            collective_id=0, has_side_effects=True, vmem_limit_bytes=63 << 20
        ),
    )(dosages, phenotypes, window_low, window_high)


def shards(dosages, phenotypes, window_low, window_high):
    found, most = packed_form(dosages, phenotypes, window_low, window_high)
    found = lax.cond(
        most[0] > CAP,
        lambda: dense(dosages, phenotypes, window_low, window_high),
        lambda: found,
    )
    return found[None]


def solution(mesh):
    placed = (P("samp", "pos"), P("samp", "pos"), P("pos"), P("pos"))
    return jax.shard_map(
        shards, mesh=mesh, in_specs=placed, out_specs=P("pos", "samp", None), check_vma=False
    )
```

```python
import functools
import math

import jax
import jax.numpy as jnp
from jax import lax
from jax.experimental import pallas as pl
from jax.experimental.pallas import tpu as pltpu
from jax.sharding import PartitionSpec as P

HALO = 512
EPS = 1e-06
MESH = pl.DeviceIdType.MESH

PIECES = (96, 48)
CAP = sum(PIECES)
QUARTER = 256
EXTRA = 8
LANES = 128
STEPS = 4
PARTS = 2


def padded(cells, sides, width):
    for axis, dim in sides:
        count = lax.axis_size(axis)
        ends = count - 1
        head = lax.slice_in_dim(cells, 0, width, axis=dim)
        tail = lax.slice_in_dim(cells, cells.shape[dim] - width, cells.shape[dim], axis=dim)
        cells = jnp.concatenate(
            [
                lax.ppermute(tail, axis, [(i, (i + 1) % count) for i in range(ends)]),
                cells,
                lax.ppermute(head, axis, [((i + 1) % count, i) for i in range(ends)]),
            ],
            axis=dim,
        )
    return cells


def from_behind(array, axis, by):
    devices = lax.axis_size(axis)
    pairs = [(i, i + by) for i in range(devices) if 0 <= i + by < devices]
    return lax.ppermute(array, axis, pairs)


def sum_squares(values):
    return jnp.sum(jnp.square(values.astype(jnp.float32)), axis=0)


def cross_rows(variant_panel, phenotypes):
    return lax.dot_general(
        variant_panel, phenotypes, (((0,), (0,)), ((), ())), preferred_element_type=jnp.float32
    )


def dense(dosages, phenotypes, window_low, window_high):
    sample_rows, block_width = dosages.shape
    peak_width = phenotypes.shape[1]
    span_width = block_width + 2 * HALO
    samp_count = lax.axis_size("samp")
    samp_index = lax.axis_index("samp")
    pos_index = lax.axis_index("pos")
    share_rows = span_width // samp_count
    own_first = samp_index * share_rows
    near_peaks = padded(phenotypes, (("pos", 1),), peak_width)
    own_tile = cross_rows(dosages, phenotypes)
    lower_edge = cross_rows(dosages[:, :HALO], near_peaks[:, :peak_width])
    upper_edge = cross_rows(dosages[:, block_width - HALO :], near_peaks[:, 2 * peak_width :])
    from_below = from_behind(upper_edge, "pos", 1)
    from_above = from_behind(lower_edge, "pos", -1)
    assembled = jnp.concatenate([from_below, own_tile, from_above], axis=0)
    owned_squares = lax.psum(sum_squares(dosages), "samp")
    peak_total = lax.psum(sum_squares(phenotypes), "samp")
    variant_total = padded(owned_squares, (("pos", 0),), HALO)
    pieces = assembled.reshape(samp_count, share_rows, peak_width)
    cross_share = jnp.sum(lax.all_to_all(pieces, "samp", 0, 0, tiled=True), axis=0)
    variant_share = lax.dynamic_slice_in_dim(variant_total, own_first, share_rows, 0)
    variant_index = (
        pos_index * block_width
        - HALO
        + own_first
        + jnp.arange(share_rows, dtype=jnp.int32)[:, None]
    )
    inside = (variant_index >= window_low[None, :]) & (variant_index <= window_high[None, :])
    factor = math.sqrt(float(sample_rows * samp_count - 2))
    scale_terms = (variant_share[:, None] + EPS) * (peak_total[None, :] + EPS)
    statistic = factor * cross_share / jnp.sqrt(scale_terms)
    return jnp.where(inside, statistic, jnp.zeros_like(statistic))


def squares_by_eight(values):
    wide = jnp.square(values.astype(jnp.float32))
    rows, columns = wide.shape
    return jnp.sum(wide.reshape(rows // EXTRA, EXTRA, columns), axis=0)


def nt(a, b):
    return lax.dot_general(a, b, (((1,), (1,)), ((), ())), preferred_element_type=jnp.float32)


def tn(a, b):
    return lax.dot_general(a, b, (((0,), (0,)), ((), ())), preferred_element_type=jnp.float32)


def nn(a, b):
    return lax.dot_general(a, b, (((1,), (0,)), ((), ())), preferred_element_type=jnp.float32)


def packed_kernel(blocks, factor, d_hbm, p_hbm, low_hbm, high_hbm, out_ref, most_ref, m, sem):
    d, p, pt, pick, own, vs8 = (m[n] for n in ("d", "p", "pt", "pick", "own", "vs8"))
    samples, variants = d.shape
    peaks = p.shape[1]
    step = samples // STEPS
    quarter = samples // PARTS
    half = variants // 2
    last = len(PIECES) - 1
    s = lax.axis_index("samp")
    b = lax.axis_index("pos")
    x = s // 2
    c = s % 2
    k = x // 2
    r = x % 2
    outer = (x == 0) | (x == 3)
    has_above = b < blocks - 1
    has_below = b > 0
    root = b == 0
    teller = (s == b // 4) & (b > 0)
    others = jnp.where(has_above, 1, 0) + jnp.where(has_below, 1, 0)
    above = (b + 1) % blocks
    below = (b + blocks - 1) % blocks
    sibling = {"samp": x * 2 + 1 - c, "pos": b}
    across = {"samp": (3 - x) * 2 + c, "pos": b}
    beside = {"samp": (x + 1 - 2 * (x % 2)) * 2 + c, "pos": b}

    def local(source, target, semaphore, i):
        rows = pl.ds(pl.multiple_of(i * step, step), step)
        return pltpu.make_async_copy(source.at[rows], target.at[rows], semaphore.at[i])

    def send(source, target, name, at, device, arrival=None):
        return pltpu.make_async_remote_copy(
            src_ref=source,
            dst_ref=target,
            send_sem=sem[name + "_send"].at[at],
            recv_sem=sem[name + "_recv"].at[at if arrival is None else arrival],
            device_id=device,
            device_id_type=MESH,
        )

    m["need_in"][...] = jnp.zeros_like(m["need_in"])
    barrier = pltpu.get_barrier_semaphore()

    def greet(samp, pos):
        pl.semaphore_signal(
            barrier, inc=1, device_id={"samp": samp, "pos": pos}, device_id_type=MESH
        )

    windows = [
        pltpu.make_async_copy(source, m[name], sem["window"].at[i])
        for i, (source, name) in enumerate(((low_hbm, "low"), (high_hbm, "high")))
    ]
    for copy in windows:
        copy.start()
    for i in range(STEPS):
        local(p_hbm, p, sem["p"], i).start()
    for i in range(1, 8):
        greet((s + i) % 8, b)
    @pl.when(root)
    def _():
        for i in range(4):

            @pl.when(s + i > 0)
            def _(i=i):
                greet(s, 4 * s + i)

    @pl.when(has_below)
    def _():
        greet(s, below)

    @pl.when(has_above)
    def _():
        greet(s, above)

    @pl.when((x == 0) & has_below)
    def _():
        for i in range(4):
            greet(2 * i + c, below)

    @pl.when((x == 3) & has_above)
    def _():
        for i in range(4):
            greet(2 * i + c, above)

    first = b * variants
    for copy in windows:
        copy.wait()
    low = m["low"][...].reshape(1, peaks)
    high = m["high"][...].reshape(1, peaks)
    before = lax.broadcasted_iota(jnp.int32, (peaks, peaks), 0) < lax.broadcasted_iota(
        jnp.int32, (peaks, peaks), 1
    )
    before = jnp.where(before, 1.0, 0.0).astype(jnp.bfloat16)
    slot = lax.broadcasted_iota(jnp.int32, (CAP, peaks), 0).astype(jnp.float32)
    count = jnp.zeros((1, 1), jnp.float32)
    for side, reach in enumerate((low < first, high >= first + variants)):
        flag = jnp.where(reach, 1.0, 0.0)
        rank = nn(jnp.broadcast_to(flag, (16, peaks)).astype(jnp.bfloat16), before)[0:1]
        rank = jnp.where(reach, rank, -1.0)
        count = jnp.maximum(count, jnp.sum(flag, axis=1, keepdims=True))
        pick[side * CAP : (side + 1) * CAP] = jnp.where(slot == rank, 1.0, 0.0).astype(
            jnp.bfloat16
        )
    m["need"][...] = jnp.broadcast_to(count, (EXTRA, LANES))

    told = m["told"]

    def tell():
        return send(m["need"], m["need_in"].at[b % 4], "need", b % 4, {"samp": s, "pos": 0})

    def heard(i):
        return send(m["need"], m["need_in"].at[i], "need", i, sibling)

    def answer(i):
        return send(m["need"], told, "answer", i, {"samp": s, "pos": 4 * s + i}, 0)

    def answer_here():
        return send(m["need"], told, "answer", 0, sibling)

    def share(i):
        return send(told, told, "share", i, {"samp": (s + i) % 8, "pos": b}, 0)

    def for_each_heard(act):
        for i in range(4):

            @pl.when(root & (s + i > 0))
            def _(i=i):
                act(i)

    to_side = (has_below, has_above)
    from_side = (has_above, has_below)

    def sel_copy(side, piece, part):
        device = {"samp": s, "pos": (below, above)[side]}
        return send(
            m["out_sel"][piece].at[side, part],
            m["in_sel"][piece].at[side, part],
            "sel",
            (piece, side, part),
            device,
        )

    def select(part, carry):
        for i in range(STEPS // PARTS):
            at = part * (STEPS // PARTS) + i
            local(p_hbm, p, sem["p"], at).wait()
            rows = pl.ds(pl.multiple_of(at * step, step), step)
            got = nt(pick[...], p[rows, :]).astype(jnp.bfloat16)
            for side in range(2):
                top = side * CAP
                for piece, size in enumerate(PIECES):
                    m["out_sel"][piece][side, part, :, i * step : (i + 1) * step] = got[
                        top : top + size
                    ]
                    top += size

        @pl.when(part == 0)
        def _():
            pl.semaphore_wait(barrier, 7 + 2 * others + jnp.where(teller, 1, 0))

            @pl.when(teller)
            def _():
                tell().start()

        for side in range(2):

            @pl.when(to_side[side])
            def _(side=side):
                sel_copy(side, 0, part).start()

        return carry

    lax.fori_loop(0, PARTS, select, 0)
    for i in range(STEPS):
        local(d_hbm, d, sem["d"], i).start()
    for piece in range(1, len(PIECES)):
        for part in range(PARTS):
            for side in range(2):

                @pl.when(to_side[side])
                def _(piece=piece, part=part, side=side):
                    sel_copy(side, piece, part).start()

    same = lax.broadcasted_iota(jnp.int32, (peaks, peaks), 0) == lax.broadcasted_iota(
        jnp.int32, (peaks, peaks), 1
    )
    same = jnp.where(same, 1.0, 0.0).astype(jnp.bfloat16)

    def turn(i, total):
        rows = pl.ds(pl.multiple_of(i * step, step), step)
        part = p[rows, :]
        pt[:, rows] = nt(same, part).astype(jnp.bfloat16)
        return total + squares_by_eight(part)

    slots = m["ps_slots"]
    slots[s, :, 0:peaks] = lax.fori_loop(
        0, STEPS, turn, jnp.zeros((EXTRA, peaks), jnp.float32)
    )

    def ps_copy(i):
        device = {"samp": (s + i) % 8, "pos": b}
        return send(slots.at[s], slots.at[s], "ps", i, device, s)

    own[...] = jnp.zeros_like(own)
    vs8[...] = jnp.zeros_like(vs8)

    def multiply(i, carry):
        local(d_hbm, d, sem["d"], i).wait()
        rows = pl.ds(pl.multiple_of(i * step, step), step)
        part = pt[:, rows]
        for q in range(4):
            columns = slice(q * QUARTER, (q + 1) * QUARTER)
            own[q % 2, q // 2, 0:peaks, :] += nn(part, d[rows, columns])
        vs8[...] += squares_by_eight(d[rows, :])
        return carry

    lax.fori_loop(0, STEPS, multiply, 0)
    for q in range(4):
        own[q % 2, q // 2, peaks : peaks + EXTRA, :] = vs8[:, q * QUARTER : (q + 1) * QUARTER]

    tall = peaks + EXTRA
    cuts = [pl.ds(0, 192), pl.ds(192, tall - 192)]
    own0, own1, own2 = m["own0"], m["own1"], m["own2"]

    def own_a(j):
        return send(own.at[1 - c, :, cuts[j]], own0.at[:, cuts[j]], "own", (0, j), sibling)

    def own_b(j):
        return send(own0.at[1 - k, cuts[j]], own1.at[cuts[j]], "own", (1, j), across)

    def own_c(j):
        return send(own1.at[cuts[j]], own2.at[cuts[j]], "own", (2, j), beside)

    def own_by_core(j):
        own_a(j).wait_recv()
        own0[:, cuts[j], :] = own0[:, cuts[j], :] + own[c, :, cuts[j], :]
        own_b(j).start()

    def own_by_chip(j):
        own_b(j).wait_recv()
        own1[cuts[j], :] = own1[cuts[j], :] + own0[k, cuts[j], :]

        @pl.when(outer)
        def _():
            own_c(j).start()

    edge, edge0, edge1, edge2, edge3 = (m[n] for n in ("edge", "edge0", "edge1", "edge2", "edge3"))

    def e0(piece):
        return send(edge[piece].at[1 - c], edge0[piece], "e0", piece, sibling)

    def e1(piece):
        return send(edge0[piece].at[1 - k], edge1[piece], "e1", piece, across)

    def rows_of(piece, which):
        size = PIECES[piece] + EXTRA
        share = edge2[piece].shape[0]
        return pl.ds(pl.multiple_of(which * (size - share), EXTRA), share)

    def e2(piece):
        return send(edge1[piece].at[rows_of(piece, 1 - r)], edge2[piece], "e2", piece, beside)

    def e3(piece):
        device = {"samp": 6 * k + c, "pos": (b + blocks + 1 - 2 * k) % blocks}
        return send(edge2[piece], edge3[piece].at[r], "e3", piece, device, (piece, r))

    def e3_from(piece, which):
        return send(
            edge2[piece], edge3[piece].at[which], "e3", piece, sibling, (piece, which)
        )

    returns = jnp.where(k == 0, has_above, has_below)

    def straight(side):
        device = {"samp": 6 * side + c, "pos": (above, below)[side]}
        return send(edge0[last].at[side], m["ends"].at[x], "ends", side, device, x)

    def edges(piece, parts):
        size = PIECES[piece]

        def part(i, carry):
            rows = pl.ds(pl.multiple_of(i * quarter, quarter), quarter)
            for side in range(2):


                @pl.when(from_side[side])
                def _(side=side):
                    sel_copy(side, piece, i).wait_recv()
                    base = half * (1 - side)
                    got = nn(m["in_sel"][piece][side, i], d[rows, base : base + half])
                    for core in range(2):
                        edge[piece][core, side, 0:size, :] += got[
                            :, core * QUARTER : (core + 1) * QUARTER
                        ]

            return carry

        lax.fori_loop(parts[0], parts[1], part, 0)

    def clear(piece):
        edge[piece][...] = jnp.zeros_like(edge[piece])

    def edges_by_core(piece):
        e0(piece).wait_recv()
        edge0[piece][...] = edge0[piece][...] + edge[piece][c]
        if piece == last:
            for side in range(2):

                @pl.when(from_side[side])
                def _(side=side):
                    straight(side).start()

        else:
            e1(piece).start()

    def edges_by_chip(piece):
        e1(piece).wait_recv()
        edge1[piece][...] = edge1[piece][...] + edge0[piece][k]
        e2(piece).start()

    def edges_by_half(piece):
        e2(piece).wait_recv()
        edge2[piece][...] = edge2[piece][...] + edge1[piece][rows_of(piece, r), :]

        @pl.when(returns)
        def _():
            e3(piece).start()

    for j in range(2):
        own_a(j).start()
    for piece in range(len(PIECES)):
        clear(piece)
    for side in range(2):
        base = half * (1 - side)
        for core in range(2):
            edge[0][core, side, PIECES[0] :, :] = vs8[
                :, base + core * QUARTER : base + (core + 1) * QUARTER
            ]
    for_each_heard(lambda i: heard(i).wait_recv())
    worst = m["need"][...]
    for i in range(4):
        worst = jnp.maximum(worst, m["need_in"][i])
    slots[s, :, peaks:] = worst
    for i in range(1, 8):
        ps_copy(i).start()
    own_by_core(0)
    own_by_core(1)
    edges(0, (0, 1))
    own_by_chip(0)
    own_by_chip(1)
    edges(0, (1, PARTS))
    e0(0).start()

    for i in range(1, 8):
        sender = (s + i) % 8
        send(slots.at[sender], slots.at[sender], "ps", i, sibling, sender).wait_recv()
    ps = slots[0, :, 0:peaks]
    worst = slots[0, :, peaks:]
    for i in range(1, 8):
        ps = ps + slots[i, :, 0:peaks]
        worst = jnp.maximum(worst, slots[i, :, peaks:])

    @pl.when(teller)
    def _():
        tell().wait_send()

    m["need"][...] = worst
    for_each_heard(lambda i: answer(i).start())
    peak_scale = factor / jnp.sqrt(jnp.sum(ps, axis=0, keepdims=True) + EPS)

    edges_by_core(0)
    edges(1, (0, 1))
    edges_by_chip(0)

    def finish(cross):
        index = (
            first
            - HALO
            + s * QUARTER
            + lax.broadcasted_iota(jnp.int32, (QUARTER, peaks), 0)
        )
        inside = (index >= low) & (index <= high)
        out_ref[...] = jnp.where(inside, cross * peak_scale, 0.0)

    def variant_scale(eight):
        return 1.0 / jnp.sqrt(jnp.sum(eight, axis=0, keepdims=True) + EPS)

    edges(1, (1, PARTS))
    e0(1).start()
    edges_by_half(0)
    edges_by_core(1)

    @pl.when(jnp.logical_not(outer))
    def _():
        for j in range(2):
            own_c(j).wait_recv()
        scale = variant_scale(own1[peaks:tall] + own2[peaks:tall])
        finish(((own1[0:peaks] + own2[0:peaks]) * scale).T)

    @pl.when(teller)
    def _():
        answer_here().wait_recv()
        for i in range(1, 8):
            share(i).start()

    @pl.when(outer)
    def _():
        for j in range(2):
            own_c(j).wait_send()

    for side in range(2):

        @pl.when((x == 3 * side) & to_side[side])
        def _(side=side):
            for which in range(2):
                e3_from(0, which).wait_recv()
            share = edge3[0].shape[1]
            size = PIECES[0]
            scale = variant_scale(edge3[0][1, share - EXTRA :])
            cross = jnp.zeros((QUARTER, peaks), jnp.float32)

            def placed(cross, rest, top):
                rest = rest * scale
                chosen = pick[top : top + rest.shape[0]]
                for _ in range(3):
                    upper = rest.astype(jnp.bfloat16)
                    cross = cross + tn(upper, chosen)
                    rest = rest - upper.astype(jnp.float32)
                return cross

            joined = m["joined"]
            joined[0:share] = edge3[0][0]
            joined[share:size] = edge3[0][1, 2 * share - size - EXTRA : share - EXTRA]
            cross = placed(cross, joined[...], side * CAP)
            for i in range(4):
                send(
                    edge0[last].at[side], m["ends"].at[i], "ends", side, sibling, i
                ).wait_recv()
            rest = m["ends"][0] + m["ends"][1] + m["ends"][2] + m["ends"][3]
            finish(placed(cross, rest, side * CAP + size))

        @pl.when((x == 3 * side) & jnp.logical_not(to_side[side]))
        def _():
            out_ref[...] = jnp.zeros((QUARTER, peaks), jnp.float32)

    @pl.when(root)
    def _():
        most_ref[0] = jnp.max(m["need"][...])

    @pl.when(jnp.logical_not(root | teller))
    def _():
        send(told, told, "share", 1, sibling, 0).wait_recv()

    @pl.when(jnp.logical_not(root))
    def _():
        most_ref[0] = jnp.max(told[...])

    def sent(part, carry):
        for side in range(2):

            @pl.when(to_side[side])
            def _(side=side):
                for piece in range(len(PIECES)):
                    sel_copy(side, piece, part).wait_send()

        return carry

    lax.fori_loop(0, PARTS, sent, 0)
    for piece in range(len(PIECES)):
        e0(piece).wait_send()
    e1(0).wait_send()
    e2(0).wait_send()

    @pl.when(returns)
    def _():
        e3(0).wait_send()

    for side in range(2):

        @pl.when(from_side[side])
        def _(side=side):
            straight(side).wait_send()

    for i in range(1, 8):
        ps_copy(i).wait_send()
    for_each_heard(lambda i: answer(i).wait_send())

    @pl.when(teller)
    def _():
        for i in range(1, 8):
            share(i).wait_send()

    for j in range(2):
        own_a(j).wait_send()
        own_b(j).wait_send()


def packed_form(dosages, phenotypes, window_low, window_high):
    samples, variants = dosages.shape
    peaks = phenotypes.shape[1]
    samp_count = lax.axis_size("samp")
    factor = math.sqrt(float(samples * samp_count - 2))
    tall = peaks + EXTRA
    f32, bf16 = jnp.float32, jnp.bfloat16
    last = len(PIECES) - 1
    sizes = [size + (EXTRA if i == 0 else 0) for i, size in enumerate(PIECES)]
    memory = {
        "d": ((samples, variants), bf16),
        "p": ((samples, peaks), bf16),
        "pt": ((peaks, samples), bf16),
        "pick": ((2 * CAP, peaks), bf16),
        "own": ((2, 2, tall, QUARTER), f32),
        "own0": ((2, tall, QUARTER), f32),
        "own1": ((tall, QUARTER), f32),
        "own2": ((tall, QUARTER), f32),
        "vs8": ((EXTRA, variants), f32),
        "ps_slots": ((8, EXTRA, peaks + LANES), f32),
        "need": ((EXTRA, LANES), f32),
        "low": ((peaks,), jnp.int32),
        "high": ((peaks,), jnp.int32),
        "told": ((EXTRA, LANES), f32),
        "need_in": ((4, EXTRA, LANES), f32),
        "joined": ((PIECES[0], QUARTER), f32),
        "ends": ((4, PIECES[last], QUARTER), f32),
    }
    memory = {name: pltpu.VMEM(*of) for name, of in memory.items()}
    for name in ("out_sel", "in_sel"):
        memory[name] = [
            pltpu.VMEM((2, PARTS, size, samples // PARTS), bf16) for size in PIECES
        ]
    memory["edge"] = [pltpu.VMEM((2, 2, size, QUARTER), f32) for size in sizes]
    memory["edge0"] = [pltpu.VMEM((2, size, QUARTER), f32) for size in sizes]
    memory["edge1"] = [pltpu.VMEM((size, QUARTER), f32) for size in sizes[:last]]
    shares = [-(-size // (2 * EXTRA)) * EXTRA for size in sizes[:last]]
    memory["edge2"] = [pltpu.VMEM((share, QUARTER), f32) for share in shares]
    memory["edge3"] = [pltpu.VMEM((2, share, QUARTER), f32) for share in shares]
    dma = pltpu.SemaphoreType.DMA
    semaphores = {"p": dma((STEPS,)), "d": dma((STEPS,))}
    for name, shape in (
        ("sel", (len(PIECES), 2, PARTS)),
        ("need", (4,)),
        ("ps", (8,)),
        ("own", (3, 2)),
        ("e0", (len(PIECES),)),
        ("e1", (last,)),
        ("e2", (last,)),
    ):
        semaphores[name + "_send"] = dma(shape)
        semaphores[name + "_recv"] = dma(shape)
    semaphores["window"] = dma((2,))
    semaphores["answer_send"] = dma((4,))
    semaphores["answer_recv"] = dma((1,))
    semaphores["share_send"] = dma((8,))
    semaphores["share_recv"] = dma((1,))
    semaphores["e3_send"] = dma((last,))
    semaphores["e3_recv"] = dma((last, 2))
    semaphores["ends_send"] = dma((2,))
    semaphores["ends_recv"] = dma((4,))
    return pl.pallas_call(
        functools.partial(packed_kernel, lax.axis_size("pos"), factor),
        out_shape=(
            jax.ShapeDtypeStruct((QUARTER, peaks), f32),
            jax.ShapeDtypeStruct((1,), f32),
        ),
        in_specs=[pl.BlockSpec(memory_space=pl.ANY)] * 4,
        out_specs=(
            pl.BlockSpec(memory_space=pltpu.VMEM),
            pl.BlockSpec(memory_space=pltpu.SMEM),
        ),
        scratch_shapes=[memory, semaphores],
        compiler_params=pltpu.CompilerParams(
            collective_id=0, has_side_effects=True, vmem_limit_bytes=63 << 20
        ),
    )(dosages, phenotypes, window_low, window_high)


def shards(dosages, phenotypes, window_low, window_high):
    found, most = packed_form(dosages, phenotypes, window_low, window_high)
    found = lax.cond(
        most[0] > CAP,
        lambda: dense(dosages, phenotypes, window_low, window_high),
        lambda: found,
    )
    return found[None]


def solution(mesh):
    placed = (P("samp", "pos"), P("samp", "pos"), P("pos"), P("pos"))
    return jax.shard_map(
        shards, mesh=mesh, in_specs=placed, out_specs=P("pos", "samp", None), check_vma=False
    )
```
